32 devices in a mesh: energy: 4 (over y, x), slab: 8 (over z, core).
Axes of the slice: x: 2, y: 2, z: 4, core: 2. Of those that a mesh axis runs over, the one named last changes fastest.
Arguments:
- left_basis: bfloat16 [8, 768, 768], P('slab'), may hold values from -0.21875 to 0.21875
- right_basis: bfloat16 [8, 768, 768], P('slab'), may hold values from -0.21875 to 0.21875
- potential_index: int32 [8], P('slab'), may hold values from 0 to 7
- levels: float32 [8, 768], replicated, may hold values from 0.8 to 1.25
- energy_values: float32 [64], replicated, may hold values from -0.1 to 0.1
- energy_weights: float32 [64], replicated, may hold values from 0.2 to 5
- energy_index: int32 [16], P('energy'), may hold values from 0 to 63
- left_source: bfloat16 [768, 128], replicated, may hold values from -6 to 6
- right_source: bfloat16 [768, 128], replicated, may hold values from -6 to 6
Outputs:
- density: float32 [8, 768], P('slab')
The draws below stay inside these ranges and needn't reach their ends.
All inputs are finite; a program needn't handle non-finite values.
Results may differ from the reference program's by a relative error of at most 0.0044.
Values may be sent and summed in bfloat16 or wider, within the bound.
A program may use at most 64 MiB of HBM per device.

```python
import math
import jax
import jax.numpy as jnp
from jax import lax

W = 768
M = 128
NPOT = 8
SLABS = 8
NE = 16
GRID = 64


def touch_ends(array, rng, low, top_value):
    index_at = [jax.random.randint(jax.random.fold_in(rng, axis), (), 0, length) for axis, length in enumerate(array.shape)]
    widest = array.shape.index(max(array.shape))
    next_to = index_at[:widest] + [(index_at[widest] + 1) % array.shape[widest]] + index_at[widest + 1:]
    return array.at[tuple(index_at)].set(low).at[tuple(next_to)].set(top_value)


def shard_levels(own_key, extent, cuts, smallest, high):
    def one(dim, shards_of):
        heights = jax.random.uniform(jax.random.fold_in(jax.random.fold_in(own_key, 6), dim), (shards_of,), jnp.float32, smallest / len(cuts), high / len(cuts))
        return jnp.repeat(jnp.exp(heights), extent[dim] // shards_of).reshape((-1,) + (1,) * (len(extent) - dim - 1))

    loudness = one(*cuts[0])
    for cut in cuts[1:]:
        loudness = loudness * one(*cut)
    return loudness


def centred(stream_key, shape, scale, bound, split=(), dtype=jnp.bfloat16):
    values = jax.random.normal(stream_key, shape, jnp.float32) * scale
    if len(split) > 0:
        values = shard_levels(stream_key, shape, split, -0.22, 0.18) * values
    return jnp.clip(values, min=-bound, max=bound).astype(dtype)


def setup_inputs(seed: int = 0) -> dict:
    streams_of = jax.random.split(jax.random.key(seed), 10)
    left_basis = centred(streams_of[0], (SLABS, W, W), W ** -0.5, 0.21875, ((0, 8),))
    right_basis = centred(streams_of[1], (SLABS, W, W), W ** -0.5, 0.21875, ((0, 8),))
    potential_index = touch_ends(jax.random.randint(streams_of[2], (SLABS,), 0, NPOT), jax.random.fold_in(streams_of[2], 1), 0, NPOT - 1).astype(jnp.int32)
    levels = jnp.clip(jax.random.uniform(streams_of[3], (NPOT, W), jnp.float32, 0.8, 1.25), 0.8, 1.25)
    energy_values = jnp.clip(jax.random.uniform(streams_of[4], (GRID,), jnp.float32, -0.1, 0.1), -0.1, 0.1)
    energy_weights = jnp.clip(jnp.exp(jax.random.uniform(streams_of[5], (GRID,), jnp.float32, math.log(0.2), math.log(5.0))), 0.2, 5.0)
    energy_index = touch_ends(jax.random.randint(streams_of[6], (NE,), 0, GRID), jax.random.fold_in(streams_of[6], 1), 0, GRID - 1).astype(jnp.int32)
    left_source = centred(streams_of[7], (W, M), 1.0, 6.0)
    right_source = centred(streams_of[8], (W, M), 1.0, 6.0)
    return {"left_basis": left_basis, "right_basis": right_basis, "potential_index": potential_index, "levels": levels, "energy_values": energy_values, "energy_weights": energy_weights, "energy_index": energy_index, "left_source": left_source, "right_source": right_source}


def reference(left_basis, right_basis, potential_index, levels, energy_values, energy_weights, energy_index, left_source, right_source):
    energy = energy_values[energy_index]
    weight = energy_weights[energy_index] / (NE * M)
    factors = 1.0 / (energy[None, :, None] - levels[potential_index][:, None, :])

    def density_of(state):
        return jnp.einsum('e,ewm->w', weight, state.astype(jnp.float32) ** 2)

    def down(state, item):
        lower, upper, scale = item
        mixed = jnp.einsum('vw,ewm->evm', upper.astype(jnp.float32), state.astype(jnp.float32))
        scaled = (scale[:, :, None] * mixed).astype(jnp.bfloat16)
        fresh = jnp.einsum('vw,ewm->evm', lower.astype(jnp.float32), scaled.astype(jnp.float32)).astype(jnp.bfloat16)
        return fresh, density_of(fresh)

    def back(state, item):
        lower, upper, scale = item
        mixed = jnp.einsum('wv,ewm->evm', lower.astype(jnp.float32), state.astype(jnp.float32))
        scaled = (scale[:, :, None] * mixed).astype(jnp.bfloat16)
        fresh = jnp.einsum('wv,ewm->evm', upper.astype(jnp.float32), scaled.astype(jnp.float32)).astype(jnp.bfloat16)
        return fresh, density_of(fresh)

    start_left = jnp.broadcast_to(left_source, (NE, W, M))
    start_right = jnp.broadcast_to(right_source, (NE, W, M))
    _, forward_part = lax.scan(down, start_left, (left_basis, right_basis, factors))
    _, backward_part = lax.scan(back, start_right, (left_basis, right_basis, factors), reverse=True)
    return forward_part + backward_part
```

```python
import functools

import jax
import jax.numpy as jnp
from jax import lax
from jax.experimental import pallas as pl
from jax.experimental.pallas import tpu as pltpu
from jax.sharding import PartitionSpec as P

MESH = pl.DeviceIdType.MESH
NN = (((1,), (0,)), ((), ()))
NT = (((1,), (1,)), ((), ()))


def dot(a, b, dims):
    return lax.dot_general(a, b, dims, preferred_element_type=jnp.float32)


def kernel(
    chain,
    teams,
    chunks,
    potential,
    energies,
    weights,
    indices,
    levels,
    left_source,
    right_source,
    left_hbm,
    right_hbm,
    out,
    left,
    right,
    first,
    density,
    gathered,
    forward_in,
    forward_out,
    backward_in,
    backward_out,
    load_sem,
    forward_send,
    forward_recv,
    backward_send,
    backward_recv,
    gather_send,
    gather_recv,
):
    count = indices.shape[0]
    orbitals = levels.shape[1]
    modes = left_source.shape[1]
    width = orbitals // chunks
    spot = lax.axis_index("slab")
    team = lax.axis_index("energy")

    loads = [
        pltpu.make_async_copy(right_hbm.at[0], right, load_sem.at[0]),
        pltpu.make_async_copy(left_hbm.at[0], left, load_sem.at[1]),
    ]
    for load in loads:
        load.start()

    barrier = pltpu.get_barrier_semaphore()

    def greet(step):
        pl.semaphore_signal(barrier, inc=1, device_id={"slab": spot + step}, device_id_type=MESH)

    pl.when(spot > 0)(lambda: greet(-1))
    pl.when(spot < chain - 1)(lambda: greet(1))
    for step in range(1, teams):
        peer = lax.rem(team + step, teams)
        pl.semaphore_signal(barrier, inc=1, device_id={"energy": peer}, device_id_type=MESH)

    row = levels[pl.ds(potential[0], 1), :]
    density[...] = jnp.zeros_like(density)

    for load in loads:
        load.wait()

    @pl.when(spot == 0)
    def _():
        source = left_source[...].astype(jnp.float32).T.astype(jnp.bfloat16)
        first[...] = dot(source, right[...], NT)

    @pl.when(spot == chain - 1)
    def _():
        source = right_source[...].astype(jnp.float32).T.astype(jnp.bfloat16)
        first[...] = dot(source, left[...], NN)

    at_end = (spot == 0) | (spot == chain - 1)
    pl.when(at_end)(lambda: pl.semaphore_wait(barrier, teams))
    pl.when(jnp.logical_not(at_end))(lambda: pl.semaphore_wait(barrier, teams + 1))

    def copy_of(source, target, send, recv, slot, chunk, step):
        return pltpu.make_async_remote_copy(
            src_ref=source.at[slot, chunk],
            dst_ref=target.at[slot, chunk],
            send_sem=send.at[slot, chunk],
            recv_sem=recv.at[slot, chunk],
            device_id={"slab": spot + step},
            device_id_type=MESH,
        )

    forward_copy = functools.partial(
        copy_of, forward_out, forward_in, forward_send, forward_recv, step=1
    )
    backward_copy = functools.partial(
        copy_of, backward_out, backward_in, backward_send, backward_recv, step=-1
    )

    def work(slot, is_first, is_last, copy, state_in, state_out, mix, spread):
        scale = 1.0 / (energies[indices[slot]] - row)
        weight = weights[indices[slot]] / (count * teams * modes)

        def finish(mixed):
            scaled = (scale * mixed).astype(jnp.bfloat16)
            for chunk in range(chunks):
                fresh = spread(scaled, chunk).astype(jnp.bfloat16)
                state_out[slot, chunk] = fresh
                pl.when(jnp.logical_not(is_last))(lambda: copy(slot, chunk).start())
            for chunk in range(chunks):
                squared = state_out[slot, chunk].astype(jnp.float32) ** 2
                part = jnp.sum(squared.reshape(modes // 8, 8, width), axis=0)
                lanes = slice(chunk * width, (chunk + 1) * width)
                density[:, lanes] += weight * part

        @pl.when(is_first)
        def _():
            finish(first[...])

        @pl.when(jnp.logical_not(is_first))
        def _():
            mixed = None
            for chunk in range(chunks):
                copy(slot, chunk).wait_recv()
                part = mix(state_in[slot, chunk], chunk)
                mixed = part if mixed is None else mixed + part
            finish(mixed)

    def lanes_of(chunk):
        return slice(chunk * width, (chunk + 1) * width)

    def turn(time, carry):
        slot = time - spot

        @pl.when((slot >= 0) & (slot < count))
        def _():
            work(
                slot,
                spot == 0,
                spot == chain - 1,
                forward_copy,
                forward_in,
                forward_out,
                lambda state, chunk: dot(state, right[:, lanes_of(chunk)], NT),
                lambda scaled, chunk: dot(scaled, left[lanes_of(chunk), :], NT),
            )

        other = time - (chain - 1 - spot)

        @pl.when((other >= 0) & (other < count))
        def _():
            work(
                other,
                spot == chain - 1,
                spot == 0,
                backward_copy,
                backward_in,
                backward_out,
                lambda state, chunk: dot(state, left[lanes_of(chunk), :], NN),
                lambda scaled, chunk: dot(scaled, right[:, lanes_of(chunk)], NN),
            )

        return carry

    lax.fori_loop(0, chain + count - 1, turn, 0)

    gathered[team] = jnp.sum(density[...], axis=0, keepdims=True)

    def share(step):
        peer = lax.rem(team + step, teams)
        return pltpu.make_async_remote_copy(
            src_ref=gathered.at[team],
            dst_ref=gathered.at[team],
            send_sem=gather_send.at[step],
            recv_sem=gather_recv.at[step],
            device_id={"energy": peer},
            device_id_type=MESH,
        )

    for step in range(1, teams):
        share(step).start()

    def settle(slot, carry):
        for chunk in range(chunks):
            pl.when(spot < chain - 1)(lambda: forward_copy(slot, chunk).wait_send())
            pl.when(spot > 0)(lambda: backward_copy(slot, chunk).wait_send())
        return carry

    lax.fori_loop(0, count, settle, 0)
    for step in range(1, teams):
        share(step).wait()
    total = gathered[0]
    for member in range(1, teams):
        total += gathered[member]
    out[...] = total


def local(
    teams,
    chain,
    left_basis,
    right_basis,
    potential_index,
    levels,
    energy_values,
    energy_weights,
    energy_index,
    left_source,
    right_source,
):
    count = energy_index.shape[0]
    orbitals = left_basis.shape[1]
    modes = left_source.shape[1]
    chunks = 3 if orbitals % 384 == 0 else 1
    block = (count, chunks, modes, orbitals // chunks)
    scalars = pl.BlockSpec(memory_space=pltpu.SMEM)
    vectors = pl.BlockSpec(memory_space=pltpu.VMEM)
    outside = pl.BlockSpec(memory_space=pl.ANY)
    copies = pltpu.SemaphoreType.DMA((count, chunks))
    return pl.pallas_call(
        functools.partial(kernel, chain, teams, chunks),
        out_shape=jax.ShapeDtypeStruct((1, orbitals), jnp.float32),
        in_specs=[scalars] * 4 + [vectors] * 3 + [outside] * 2,
        out_specs=vectors,
        scratch_shapes=[
            pltpu.VMEM((orbitals, orbitals), jnp.bfloat16),
            pltpu.VMEM((orbitals, orbitals), jnp.bfloat16),
            pltpu.VMEM((modes, orbitals), jnp.float32),
            pltpu.VMEM((8, orbitals), jnp.float32),
            pltpu.VMEM((teams, 1, orbitals), jnp.float32),
            pltpu.VMEM(block, jnp.bfloat16),
            pltpu.VMEM(block, jnp.bfloat16),
            pltpu.VMEM(block, jnp.bfloat16),
            pltpu.VMEM(block, jnp.bfloat16),
            pltpu.SemaphoreType.DMA((2,)),
            copies,
            copies,
            copies,
            copies,
            pltpu.SemaphoreType.DMA((teams,)),
            pltpu.SemaphoreType.DMA((teams,)),
        ],
        compiler_params=pltpu.CompilerParams(
            collective_id=0, has_side_effects=True, vmem_limit_bytes=32 << 20
        ),
    )(
        potential_index,
        energy_values,
        energy_weights,
        energy_index,
        levels,
        left_source,
        right_source,
        left_basis,
        right_basis,
    )


def solution(mesh):
    placed = (
        P("slab", None, None),
        P("slab", None, None),
        P("slab"),
        P(),
        P(),
        P(),
        P("energy"),
        P(),
        P(),
    )
    return jax.shard_map(
        functools.partial(local, mesh.shape["energy"], mesh.shape["slab"]),
        mesh=mesh,
        in_specs=placed,
        out_specs=P("slab", None),
        check_vma=False,
    )
```

```python
import functools

import jax
import jax.numpy as jnp
from jax import lax
from jax.experimental import pallas as pl
from jax.experimental.pallas import tpu as pltpu
from jax.sharding import PartitionSpec as P

MESH = pl.DeviceIdType.MESH
NN = (((1,), (0,)), ((), ()))
NT = (((1,), (1,)), ((), ()))


def dot(a, b, dims):
    return lax.dot_general(a, b, dims, preferred_element_type=jnp.float32)


def kernel(
    chain,
    teams,
    chunks,
    potential,
    energies_hbm,
    weights_hbm,
    indices_hbm,
    levels_hbm,
    left_source_hbm,
    right_source_hbm,
    left_hbm,
    right_hbm,
    out,
    energies,
    weights,
    indices,
    levels,
    source,
    left,
    right,
    left_turned,
    right_turned,
    first,
    density,
    gathered,
    forward_in,
    forward_out,
    backward_in,
    backward_out,
    load_sem,
    forward_send,
    forward_recv,
    backward_send,
    backward_recv,
    gather_send,
    gather_recv,
):
    count = indices.shape[0]
    orbitals = levels.shape[1]
    modes = source.shape[1]
    width = orbitals // chunks
    spot = lax.axis_index("slab")
    team = lax.axis_index("energy")

    def load(origin, target, place):
        return pltpu.make_async_copy(origin, target, load_sem.at[place])

    left_load = load(left_source_hbm, source, 0)
    right_load = load(right_source_hbm, source, 0)
    bases = [load(right_hbm.at[0], right, 1), load(left_hbm.at[0], left, 2)]
    tables = [
        load(energies_hbm, energies, 4),
        load(weights_hbm, weights, 5),
        load(indices_hbm, indices, 6),
        load(levels_hbm, levels, 7),
    ]
    pl.when(spot == 0)(left_load.start)
    pl.when(spot == chain - 1)(right_load.start)
    for item in bases + tables:
        item.start()

    barrier = pltpu.get_barrier_semaphore()

    def greet(step):
        pl.semaphore_signal(barrier, inc=1, device_id={"slab": spot + step}, device_id_type=MESH)

    pl.when(spot > 0)(lambda: greet(-1))
    pl.when(spot < chain - 1)(lambda: greet(1))
    for step in range(1, teams):
        peer = lax.rem(team + step, teams)
        pl.semaphore_signal(barrier, inc=1, device_id={"energy": peer}, device_id_type=MESH)

    density[...] = jnp.zeros_like(density)
    for item in bases:
        item.wait()

    def turned_source():
        return source[...].astype(jnp.float32).T.astype(jnp.bfloat16)

    @pl.when(spot == 0)
    def _():
        left_load.wait()
        first[...] = dot(turned_source(), right[...], NT)

    @pl.when(spot == chain - 1)
    def _():
        right_load.wait()
        first[...] = dot(turned_source(), left[...], NN)

    def turn_bases():
        for chunk in range(chunks):
            rows = slice(chunk * width, (chunk + 1) * width)
            left_turned[rows, :] = left[:, rows].T
            right_turned[rows, :] = right[:, rows].T

    pl.when((spot > 0) & (spot < chain - 1))(turn_bases)
    for item in tables:
        item.wait()
    row = levels[pl.ds(potential[0], 1), :]

    at_end = (spot == 0) | (spot == chain - 1)
    pl.when(at_end)(lambda: pl.semaphore_wait(barrier, teams))
    pl.when(jnp.logical_not(at_end))(lambda: pl.semaphore_wait(barrier, teams + 1))

    def copy_of(source, target, send, recv, slot, chunk, step):
        return pltpu.make_async_remote_copy(
            src_ref=source.at[slot, chunk],
            dst_ref=target.at[slot, chunk],
            send_sem=send.at[slot, chunk],
            recv_sem=recv.at[slot, chunk],
            device_id={"slab": spot + step},
            device_id_type=MESH,
        )

    forward_copy = functools.partial(
        copy_of, forward_out, forward_in, forward_send, forward_recv, step=1
    )
    backward_copy = functools.partial(
        copy_of, backward_out, backward_in, backward_send, backward_recv, step=-1
    )

    def work(slot, is_first, is_last, copy, state_in, state_out, mix, spread, first_spread):
        scale = 1.0 / (energies[indices[slot]] - row)
        weight = weights[indices[slot]] / (count * teams * modes)

        def finish(mixed, spread):
            scaled = (scale * mixed).astype(jnp.bfloat16)
            for chunk in range(chunks):
                fresh = spread(scaled, chunk).astype(jnp.bfloat16)
                state_out[slot, chunk] = fresh
                pl.when(jnp.logical_not(is_last))(lambda: copy(slot, chunk).start())
            for chunk in range(chunks):
                squared = state_out[slot, chunk].astype(jnp.float32) ** 2
                part = jnp.sum(squared.reshape(modes // 8, 8, width), axis=0)
                lanes = slice(chunk * width, (chunk + 1) * width)
                density[:, lanes] += weight * part

        @pl.when(is_first)
        def _():
            finish(first[...], first_spread)

        @pl.when(jnp.logical_not(is_first))
        def _():
            mixed = None
            for chunk in range(chunks):
                copy(slot, chunk).wait_recv()
                part = mix(state_in[slot, chunk], chunk)
                mixed = part if mixed is None else mixed + part
            finish(mixed, spread)

    def lanes_of(chunk):
        return slice(chunk * width, (chunk + 1) * width)

    def turn(time, carry):
        idle = min(count, chain - 1)
        pl.when((spot == chain - 1) & (time == idle))(turn_bases)
        slot = time - spot

        @pl.when((slot >= 0) & (slot < count))
        def _():
            work(
                slot,
                spot == 0,
                spot == chain - 1,
                forward_copy,
                forward_in,
                forward_out,
                lambda state, chunk: dot(state, right_turned[lanes_of(chunk), :], NN),
                lambda scaled, chunk: dot(scaled, left_turned[:, lanes_of(chunk)], NN),
                lambda scaled, chunk: dot(scaled, left[lanes_of(chunk), :], NT),
            )

        other = time - (chain - 1 - spot)

        @pl.when((other >= 0) & (other < count))
        def _():
            work(
                other,
                spot == chain - 1,
                spot == 0,
                backward_copy,
                backward_in,
                backward_out,
                lambda state, chunk: dot(state, left[lanes_of(chunk), :], NN),
                lambda scaled, chunk: dot(scaled, right[:, lanes_of(chunk)], NN),
                lambda scaled, chunk: dot(scaled, right[:, lanes_of(chunk)], NN),
            )

        return carry

    lax.fori_loop(0, chain + count - 1, turn, 0)

    gathered[team] = jnp.sum(density[...], axis=0, keepdims=True)

    def share(step):
        peer = lax.rem(team + step, teams)
        return pltpu.make_async_remote_copy(
            src_ref=gathered.at[team],
            dst_ref=gathered.at[team],
            send_sem=gather_send.at[step],
            recv_sem=gather_recv.at[step],
            device_id={"energy": peer},
            device_id_type=MESH,
        )

    for step in range(1, teams):
        share(step).start()

    def settle(slot, carry):
        for chunk in range(chunks):
            pl.when(spot < chain - 1)(lambda: forward_copy(slot, chunk).wait_send())
            pl.when(spot > 0)(lambda: backward_copy(slot, chunk).wait_send())
        return carry

    lax.fori_loop(0, count, settle, 0)
    for step in range(1, teams):
        share(step).wait()
    total = gathered[0]
    for member in range(1, teams):
        total += gathered[member]
    out[...] = total


def local(
    teams,
    chain,
    left_basis,
    right_basis,
    potential_index,
    levels,
    energy_values,
    energy_weights,
    energy_index,
    left_source,
    right_source,
):
    count = energy_index.shape[0]
    orbitals = left_basis.shape[1]
    modes = left_source.shape[1]
    chunks = 3 if orbitals % 384 == 0 else 1
    block = (count, chunks, modes, orbitals // chunks)
    outside = pl.BlockSpec(memory_space=pltpu.HBM)
    square = pltpu.VMEM((orbitals, orbitals), jnp.bfloat16)
    copies = pltpu.SemaphoreType.DMA((count, chunks))
    return pl.pallas_call(
        functools.partial(kernel, chain, teams, chunks),
        out_shape=jax.ShapeDtypeStruct((1, orbitals), jnp.float32),
        in_specs=[pl.BlockSpec(memory_space=pltpu.SMEM)] + [outside] * 8,
        out_specs=pl.BlockSpec(memory_space=pltpu.VMEM),
        scratch_shapes=[
            pltpu.SMEM(energy_values.shape, jnp.float32),
            pltpu.SMEM(energy_weights.shape, jnp.float32),
            pltpu.SMEM(energy_index.shape, jnp.int32),
            pltpu.VMEM(levels.shape, jnp.float32),
            pltpu.VMEM(left_source.shape, jnp.bfloat16),
            square,
            square,
            square,
            square,
            pltpu.VMEM((modes, orbitals), jnp.float32),
            pltpu.VMEM((8, orbitals), jnp.float32),
            pltpu.VMEM((teams, 1, orbitals), jnp.float32),
            pltpu.VMEM(block, jnp.bfloat16),
            pltpu.VMEM(block, jnp.bfloat16),
            pltpu.VMEM(block, jnp.bfloat16),
            pltpu.VMEM(block, jnp.bfloat16),
            pltpu.SemaphoreType.DMA((8,)),
            copies,
            copies,
            copies,
            copies,
            pltpu.SemaphoreType.DMA((teams,)),
            pltpu.SemaphoreType.DMA((teams,)),
        ],
        compiler_params=pltpu.CompilerParams(
            collective_id=0, has_side_effects=True, vmem_limit_bytes=63 << 20
        ),
    )(
        potential_index,
        energy_values,
        energy_weights,
        energy_index,
        levels,
        left_source,
        right_source,
        left_basis,
        right_basis,
    )


def solution(mesh):
    placed = (
        P("slab", None, None),
        P("slab", None, None),
        P("slab"),
        P(),
        P(),
        P(),
        P("energy"),
        P(),
        P(),
    )
    return jax.shard_map(
        functools.partial(local, mesh.shape["energy"], mesh.shape["slab"]),
        mesh=mesh,
        in_specs=placed,
        out_specs=P("slab", None),
        check_vma=False,
    )
```

```python
import functools

import jax
import jax.numpy as jnp
from jax import lax
from jax.experimental import pallas as pl
from jax.experimental.pallas import tpu as pltpu
from jax.sharding import PartitionSpec as P

MESH = pl.DeviceIdType.MESH
NN = (((1,), (0,)), ((), ()))
NT = (((1,), (1,)), ((), ()))


def dot(a, b, dims):
    return lax.dot_general(a, b, dims, preferred_element_type=jnp.float32)


def kernel(
    chain,
    teams,
    chunks,
    potential,
    energies_hbm,
    weights_hbm,
    indices_hbm,
    levels_hbm,
    left_source_hbm,
    right_source_hbm,
    left_hbm,
    right_hbm,
    out,
    energies,
    weights,
    indices,
    levels,
    source,
    left,
    right,
    left_turned,
    right_turned,
    first,
    density,
    gathered,
    forward_in,
    forward_out,
    backward_in,
    backward_out,
    load_sem,
    forward_send,
    forward_recv,
    backward_send,
    backward_recv,
    gather_send,
    gather_recv,
):
    count = indices.shape[0]
    orbitals = levels.shape[1]
    modes = source.shape[1]
    width = orbitals // chunks
    spot = lax.axis_index("slab")
    team = lax.axis_index("energy")

    def load(origin, target, place):
        return pltpu.make_async_copy(origin, target, load_sem.at[place])

    left_load = load(left_source_hbm, source, 0)
    right_load = load(right_source_hbm, source, 0)
    bases = [load(right_hbm.at[0], right, 1), load(left_hbm.at[0], left, 2)]
    tables = [
        load(energies_hbm, energies, 4),
        load(weights_hbm, weights, 5),
        load(indices_hbm, indices, 6),
        load(levels_hbm, levels, 7),
    ]
    pl.when(spot == 0)(left_load.start)
    pl.when(spot == chain - 1)(right_load.start)
    for item in bases + tables:
        item.start()

    barrier = pltpu.get_barrier_semaphore()

    def greet(step):
        pl.semaphore_signal(barrier, inc=1, device_id={"slab": spot + step}, device_id_type=MESH)

    pl.when(spot > 0)(lambda: greet(-1))
    pl.when(spot < chain - 1)(lambda: greet(1))
    for step in range(1, teams):
        peer = lax.rem(team + step, teams)
        pl.semaphore_signal(barrier, inc=1, device_id={"energy": peer}, device_id_type=MESH)

    density[...] = jnp.zeros_like(density)

    def turned_source():
        return source[...].astype(jnp.float32).T.astype(jnp.bfloat16)

    @pl.when(spot == 0)
    def _():
        left_load.wait()
        bases[0].wait()
        first[...] = dot(turned_source(), right[...], NT)

    @pl.when(spot == chain - 1)
    def _():
        right_load.wait()
        bases[1].wait()
        first[...] = dot(turned_source(), left[...], NN)

    def turn_bases():
        for chunk in range(chunks):
            rows = slice(chunk * width, (chunk + 1) * width)
            left_turned[rows, :] = left[:, rows].T
            right_turned[rows, :] = right[:, rows].T

    pl.when(spot == 0)(bases[1].wait)
    pl.when(spot == chain - 1)(bases[0].wait)

    @pl.when((spot > 0) & (spot < chain - 1))
    def _():
        for item in bases:
            item.wait()
        turn_bases()

    for item in tables:
        item.wait()
    row = levels[pl.ds(potential[0], 1), :]

    at_end = (spot == 0) | (spot == chain - 1)
    pl.when(at_end)(lambda: pl.semaphore_wait(barrier, teams))
    pl.when(jnp.logical_not(at_end))(lambda: pl.semaphore_wait(barrier, teams + 1))

    def copy_of(source, target, send, recv, slot, chunk, step):
        return pltpu.make_async_remote_copy(
            src_ref=source.at[slot, chunk],
            dst_ref=target.at[slot, chunk],
            send_sem=send.at[slot, chunk],
            recv_sem=recv.at[slot, chunk],
            device_id={"slab": spot + step},
            device_id_type=MESH,
        )

    forward_copy = functools.partial(
        copy_of, forward_out, forward_in, forward_send, forward_recv, step=1
    )
    backward_copy = functools.partial(
        copy_of, backward_out, backward_in, backward_send, backward_recv, step=-1
    )

    def work(slot, is_first, is_last, copy, state_in, state_out, mix, spread, first_spread):
        scale = 1.0 / (energies[indices[slot]] - row)
        weight = weights[indices[slot]] / (count * teams * modes)

        def finish(mixed, spread):
            scaled = (scale * mixed).astype(jnp.bfloat16)
            for chunk in range(chunks):
                fresh = spread(scaled, chunk).astype(jnp.bfloat16)
                state_out[slot, chunk] = fresh
                pl.when(jnp.logical_not(is_last))(lambda: copy(slot, chunk).start())
            for chunk in range(chunks):
                squared = state_out[slot, chunk].astype(jnp.float32) ** 2
                part = jnp.sum(squared.reshape(modes // 8, 8, width), axis=0)
                lanes = slice(chunk * width, (chunk + 1) * width)
                density[:, lanes] += weight * part

        @pl.when(is_first)
        def _():
            finish(first[...], first_spread)

        @pl.when(jnp.logical_not(is_first))
        def _():
            mixed = None
            for chunk in range(chunks):
                copy(slot, chunk).wait_recv()
                part = mix(state_in[slot, chunk], chunk)
                mixed = part if mixed is None else mixed + part
            finish(mixed, spread)

    def lanes_of(chunk):
        return slice(chunk * width, (chunk + 1) * width)

    def forward(time, wanted):
        slot = time - spot

        @pl.when(wanted & (slot >= 0) & (slot < count))
        def _():
            work(
                slot,
                spot == 0,
                spot == chain - 1,
                forward_copy,
                forward_in,
                forward_out,
                lambda state, chunk: dot(state, right_turned[lanes_of(chunk), :], NN),
                lambda scaled, chunk: dot(scaled, left_turned[:, lanes_of(chunk)], NN),
                lambda scaled, chunk: dot(scaled, left[lanes_of(chunk), :], NT),
            )

    def backward(time):
        other = time - (chain - 1 - spot)

        @pl.when((other >= 0) & (other < count))
        def _():
            work(
                other,
                spot == chain - 1,
                spot == 0,
                backward_copy,
                backward_in,
                backward_out,
                lambda state, chunk: dot(state, left[lanes_of(chunk), :], NN),
                lambda scaled, chunk: dot(scaled, right[:, lanes_of(chunk)], NN),
                lambda scaled, chunk: dot(scaled, right[:, lanes_of(chunk)], NN),
            )

    def turn(time, carry):
        idle = min(count, chain - 1)
        pl.when((spot == chain - 1) & (time == idle))(turn_bases)
        forward(time, spot < chain // 2)
        backward(time)
        forward(time, spot >= chain // 2)
        return carry

    lax.fori_loop(0, chain + count - 1, turn, 0)

    gathered[team] = jnp.sum(density[...], axis=0, keepdims=True)

    def share(step):
        peer = lax.rem(team + step, teams)
        return pltpu.make_async_remote_copy(
            src_ref=gathered.at[team],
            dst_ref=gathered.at[team],
            send_sem=gather_send.at[step],
            recv_sem=gather_recv.at[step],
            device_id={"energy": peer},
            device_id_type=MESH,
        )

    for step in range(1, teams):
        share(step).start()

    def settle(slot, carry):
        for chunk in range(chunks):
            pl.when(spot < chain - 1)(lambda: forward_copy(slot, chunk).wait_send())
            pl.when(spot > 0)(lambda: backward_copy(slot, chunk).wait_send())
        return carry

    lax.fori_loop(0, count, settle, 0)
    for step in range(1, teams):
        share(step).wait()
    total = gathered[0]
    for member in range(1, teams):
        total += gathered[member]
    out[...] = total


def local(
    teams,
    chain,
    left_basis,
    right_basis,
    potential_index,
    levels,
    energy_values,
    energy_weights,
    energy_index,
    left_source,
    right_source,
):
    count = energy_index.shape[0]
    orbitals = left_basis.shape[1]
    modes = left_source.shape[1]
    chunks = 1
    block = (count, chunks, modes, orbitals // chunks)
    outside = pl.BlockSpec(memory_space=pltpu.HBM)
    square = pltpu.VMEM((orbitals, orbitals), jnp.bfloat16)
    copies = pltpu.SemaphoreType.DMA((count, chunks))
    return pl.pallas_call(
        functools.partial(kernel, chain, teams, chunks),
        out_shape=jax.ShapeDtypeStruct((1, orbitals), jnp.float32),
        in_specs=[pl.BlockSpec(memory_space=pltpu.SMEM)] + [outside] * 8,
        out_specs=pl.BlockSpec(memory_space=pltpu.VMEM),
        scratch_shapes=[
            pltpu.SMEM(energy_values.shape, jnp.float32),
            pltpu.SMEM(energy_weights.shape, jnp.float32),
            pltpu.SMEM(energy_index.shape, jnp.int32),
            pltpu.VMEM(levels.shape, jnp.float32),
            pltpu.VMEM(left_source.shape, jnp.bfloat16),
            square,
            square,
            square,
            square,
            pltpu.VMEM((modes, orbitals), jnp.float32),
            pltpu.VMEM((8, orbitals), jnp.float32),
            pltpu.VMEM((teams, 1, orbitals), jnp.float32),
            pltpu.VMEM(block, jnp.bfloat16),
            pltpu.VMEM(block, jnp.bfloat16),
            pltpu.VMEM(block, jnp.bfloat16),
            pltpu.VMEM(block, jnp.bfloat16),
            pltpu.SemaphoreType.DMA((8,)),
            copies,
            copies,
            copies,
            copies,
            pltpu.SemaphoreType.DMA((teams,)),
            pltpu.SemaphoreType.DMA((teams,)),
        ],
        compiler_params=pltpu.CompilerParams(
            collective_id=0, has_side_effects=True, vmem_limit_bytes=63 << 20
        ),
    )(
        potential_index,
        energy_values,
        energy_weights,
        energy_index,
        levels,
        left_source,
        right_source,
        left_basis,
        right_basis,
    )


def solution(mesh):
    placed = (
        P("slab", None, None),
        P("slab", None, None),
        P("slab"),
        P(),
        P(),
        P(),
        P("energy"),
        P(),
        P(),
    )
    return jax.shard_map(
        functools.partial(local, mesh.shape["energy"], mesh.shape["slab"]),
        mesh=mesh,
        in_specs=placed,
        out_specs=P("slab", None),
        check_vma=False,
    )
```

```python
import functools

import jax
import jax.numpy as jnp
from jax import lax
from jax.experimental import pallas as pl
from jax.experimental.pallas import tpu as pltpu
from jax.sharding import PartitionSpec as P

MESH = pl.DeviceIdType.MESH
NN = (((1,), (0,)), ((), ()))
NT = (((1,), (1,)), ((), ()))


def dot(a, b, dims):
    return lax.dot_general(a, b, dims, preferred_element_type=jnp.float32)


def kernel(
    chain,
    teams,
    potential,
    energies_hbm,
    weights_hbm,
    indices_hbm,
    levels_hbm,
    left_source_hbm,
    right_source_hbm,
    left_hbm,
    right_hbm,
    out,
    energies,
    weights,
    indices,
    levels,
    source,
    left,
    right,
    left_turned,
    right_turned,
    rows,
    first,
    middle,
    density,
    partial,
    gathered,
    forward_in,
    forward_out,
    backward_in,
    backward_out,
    load_sem,
    swap_send,
    swap_recv,
    forward_send,
    forward_recv,
    backward_send,
    backward_recv,
    gather_send,
    gather_recv,
):
    count = indices.shape[0]
    modes = source.shape[1]
    orbitals = levels.shape[1]
    spot = lax.axis_index("slab")
    team = lax.axis_index("energy")
    chips = chain // 2
    chip = spot // 2
    core = spot % 2
    twin = spot + 1 - 2 * core
    lowest = chip == 0
    highest = chip == chips - 1

    def load(origin, target, place):
        return pltpu.make_async_copy(origin, target, load_sem.at[place])

    left_load = load(left_source_hbm, source, 0)
    right_load = load(right_source_hbm, source, 0)
    bases = [
        load(right_hbm.at[0], right.at[core], 1),
        load(left_hbm.at[0], left.at[core], 2),
    ]
    tables = [
        load(energies_hbm, energies, 3),
        load(weights_hbm, weights, 4),
        load(indices_hbm, indices, 5),
        load(levels_hbm, levels, 6),
    ]
    pl.when(spot == 0)(left_load.start)
    pl.when(spot == chain - 1)(right_load.start)
    for item in bases + tables:
        item.start()

    barrier = pltpu.get_barrier_semaphore()

    def greet(place):
        pl.semaphore_signal(barrier, inc=1, device_id=place, device_id_type=MESH)

    def greet_chip(other):
        greet({"slab": 2 * other})
        greet({"slab": 2 * other + 1})

    pl.when(chip > 0)(lambda: greet_chip(chip - 1))
    pl.when(chip < chips - 1)(lambda: greet_chip(chip + 1))
    greet({"slab": twin})
    for step in range(1, teams):
        peer = lax.rem(team + step, teams)
        greet({"energy": peer})
        greet({"energy": peer, "slab": twin})

    density[...] = jnp.zeros_like(density)
    for item in tables:
        item.wait()
    rows[core] = levels[pl.ds(potential[0], 1), :]

    at_end = lowest | highest
    pl.when(at_end)(lambda: pl.semaphore_wait(barrier, 2 * teams + 1))
    pl.when(jnp.logical_not(at_end))(lambda: pl.semaphore_wait(barrier, 2 * teams + 3))

    def swap(origin, target, place):
        return pltpu.make_async_remote_copy(
            src_ref=origin,
            dst_ref=target,
            send_sem=swap_send.at[place],
            recv_sem=swap_recv.at[place],
            device_id={"slab": twin},
            device_id_type=MESH,
        )

    swaps = [
        swap(rows.at[core], rows.at[core], 0),
        swap(right_hbm.at[0], right.at[core], 1),
        swap(left_hbm.at[0], left.at[core], 2),
    ]
    for item in swaps:
        item.start()
    for item in bases:
        item.wait()

    def turned_source():
        return source[...].astype(jnp.float32).T.astype(jnp.bfloat16)

    @pl.when(spot == 0)
    def _():
        left_load.wait()
        first[...] = dot(turned_source(), right[0], NT)

    @pl.when(spot == chain - 1)
    def _():
        right_load.wait()
        first[...] = dot(turned_source(), left[1], NN)

    def turn_bases(side):
        left_turned[side] = left[side].T
        right_turned[side] = right[side].T

    def turn_both():
        turn_bases(0)
        turn_bases(1)

    def settle_swaps():
        for item in swaps:
            item.wait_recv()

    pl.when(spot == 1)(lambda: turn_bases(1))

    @pl.when(jnp.logical_not(at_end))
    def _():
        settle_swaps()
        turn_both()

    def copy_of(origin, target, send, recv, slot, place):
        return pltpu.make_async_remote_copy(
            src_ref=origin.at[slot],
            dst_ref=target.at[slot],
            send_sem=send.at[slot],
            recv_sem=recv.at[slot],
            device_id={"slab": place},
            device_id_type=MESH,
        )

    forward_copy = functools.partial(
        copy_of, forward_out, forward_in, forward_send, forward_recv
    )
    backward_copy = functools.partial(
        copy_of, backward_out, backward_in, backward_send, backward_recv
    )

    def scaled(mixed, slot, side):
        scale = 1.0 / (energies[indices[slot]] - rows[side])
        return (scale * mixed).astype(jnp.bfloat16)

    def count_in(state, slot, side):
        weight = weights[indices[slot]] / (count * teams * modes)
        squared = state[...].astype(jnp.float32) ** 2
        part = jnp.sum(squared.reshape(modes // 8, 8, orbitals), axis=0)
        density[side] += weight * part

    def down(state, slot, side):
        mixed = dot(state, right_turned[side], NN)
        return dot(scaled(mixed, slot, side), left_turned[side], NN).astype(jnp.bfloat16)

    def up(state, slot, side):
        mixed = dot(state, left[side], NN)
        return dot(scaled(mixed, slot, side), right[side], NN).astype(jnp.bfloat16)

    def each(body):
        def step(slot, carry):
            body(slot)
            return carry

        lax.fori_loop(0, count, step, 0)

    def mine(body):
        each(lambda slot: pl.when(slot % 2 == core)(lambda: body(slot)))

    def sweep(begin, end, near, far, copy, state_in, state_out, advance, opening, start, onward):
        @pl.when(begin & (core == near))
        def _():
            def body(slot):
                mixed = scaled(first[...], slot, near)
                state_out[slot] = opening(mixed).astype(jnp.bfloat16)
                copy(slot, twin).start()
                count_in(state_out.at[slot], slot, near)

            each(body)

        @pl.when(begin & (core == far))
        def _():
            def body(slot):
                copy(slot, twin).wait_recv()
                state_out[slot] = advance(state_in[slot], slot, far)
                copy(slot, start + slot % 2).start()
                count_in(state_out.at[slot], slot, far)

            each(body)

        @pl.when(jnp.logical_not(begin))
        def _():
            def body(slot):
                copy(slot, twin).wait_recv()
                middle[...] = advance(state_in[slot], slot, near)
                state_out[slot] = advance(middle[...], slot, far)
                pl.when(jnp.logical_not(end))(lambda: copy(slot, onward).start())
                count_in(middle, slot, near)
                count_in(state_out.at[slot], slot, far)

            mine(body)

    def forward():
        sweep(
            lowest, highest, 0, 1, forward_copy, forward_in, forward_out, down,
            lambda mixed: dot(mixed, left[0], NT), 2, spot + 2,
        )

    def backward():
        sweep(
            highest, lowest, 1, 0, backward_copy, backward_in, backward_out, up,
            lambda mixed: dot(mixed, right[1], NN), chain - 4, spot - 2,
        )

    upper = chip >= chips // 2
    pl.when(jnp.logical_not(upper))(forward)
    pl.when(lowest)(settle_swaps)
    backward()

    @pl.when(highest)
    def _():
        settle_swaps()
        turn_both()

    pl.when(upper)(forward)

    gathered[2 * team + core] = jnp.sum(density[core], axis=0, keepdims=True)
    partial[...] = jnp.sum(density[1 - core], axis=0, keepdims=True)

    def share(step, across):
        peer = lax.rem(team + step, teams)
        place = teams * across + step
        return pltpu.make_async_remote_copy(
            src_ref=partial if across else gathered.at[2 * team + core],
            dst_ref=gathered.at[2 * team + core],
            send_sem=gather_send.at[place],
            recv_sem=gather_recv.at[place],
            device_id={"energy": peer, "slab": twin if across else spot},
            device_id_type=MESH,
        )

    shares = [share(step, 1) for step in range(teams)]
    shares += [share(step, 0) for step in range(1, teams)]
    for item in shares:
        item.start()

    def sent(copy, begin, end):
        pl.when(begin)(lambda: each(lambda slot: copy(slot, twin).wait_send()))
        pl.when(jnp.logical_not(begin | end))(
            lambda: mine(lambda slot: copy(slot, twin).wait_send())
        )

    sent(forward_copy, lowest, highest)
    sent(backward_copy, highest, lowest)
    for item in swaps:
        item.wait_send()
    for item in shares:
        item.wait()
    total = gathered[0]
    for member in range(1, 2 * teams):
        total += gathered[member]
    out[...] = total


def local(
    teams,
    chain,
    left_basis,
    right_basis,
    potential_index,
    levels,
    energy_values,
    energy_weights,
    energy_index,
    left_source,
    right_source,
):
    count = energy_index.shape[0]
    orbitals = left_basis.shape[1]
    modes = left_source.shape[1]
    block = (count, modes, orbitals)
    outside = pl.BlockSpec(memory_space=pltpu.HBM)
    square = pltpu.VMEM((2, orbitals, orbitals), jnp.bfloat16)
    copies = pltpu.SemaphoreType.DMA((count,))
    return pl.pallas_call(
        functools.partial(kernel, chain, teams),
        out_shape=jax.ShapeDtypeStruct((1, orbitals), jnp.float32),
        in_specs=[pl.BlockSpec(memory_space=pltpu.SMEM)] + [outside] * 8,
        out_specs=pl.BlockSpec(memory_space=pltpu.VMEM),
        scratch_shapes=[
            pltpu.SMEM(energy_values.shape, jnp.float32),
            pltpu.SMEM(energy_weights.shape, jnp.float32),
            pltpu.SMEM(energy_index.shape, jnp.int32),
            pltpu.VMEM(levels.shape, jnp.float32),
            pltpu.VMEM(left_source.shape, jnp.bfloat16),
            square,
            square,
            square,
            square,
            pltpu.VMEM((2, 1, orbitals), jnp.float32),
            pltpu.VMEM((modes, orbitals), jnp.float32),
            pltpu.VMEM((modes, orbitals), jnp.bfloat16),
            pltpu.VMEM((2, 8, orbitals), jnp.float32),
            pltpu.VMEM((1, orbitals), jnp.float32),
            pltpu.VMEM((2 * teams, 1, orbitals), jnp.float32),
            pltpu.VMEM(block, jnp.bfloat16),
            pltpu.VMEM(block, jnp.bfloat16),
            pltpu.VMEM(block, jnp.bfloat16),
            pltpu.VMEM(block, jnp.bfloat16),
            pltpu.SemaphoreType.DMA((7,)),
            pltpu.SemaphoreType.DMA((3,)),
            pltpu.SemaphoreType.DMA((3,)),
            copies,
            copies,
            copies,
            copies,
            pltpu.SemaphoreType.DMA((2 * teams,)),
            pltpu.SemaphoreType.DMA((2 * teams,)),
        ],
        compiler_params=pltpu.CompilerParams(
            collective_id=0, has_side_effects=True, vmem_limit_bytes=63 << 20
        ),
    )(
        potential_index,
        energy_values,
        energy_weights,
        energy_index,
        levels,
        left_source,
        right_source,
        left_basis,
        right_basis,
    )


def solution(mesh):
    placed = (
        P("slab", None, None),
        P("slab", None, None),
        P("slab"),
        P(),
        P(),
        P(),
        P("energy"),
        P(),
        P(),
    )
    return jax.shard_map(
        functools.partial(local, mesh.shape["energy"], mesh.shape["slab"]),
        mesh=mesh,
        in_specs=placed,
        out_specs=P("slab", None),
        check_vma=False,
    )
```

```python
import functools

import jax
import jax.numpy as jnp
from jax import lax
from jax.experimental import pallas as pl
from jax.experimental.pallas import tpu as pltpu
from jax.sharding import PartitionSpec as P

MESH = pl.DeviceIdType.MESH
NN = (((1,), (0,)), ((), ()))
NT = (((1,), (1,)), ((), ()))


def dot(a, b, dims):
    return lax.dot_general(a, b, dims, preferred_element_type=jnp.float32)


def kernel(
    chain,
    teams,
    potential,
    energies_hbm,
    weights_hbm,
    indices_hbm,
    levels_hbm,
    left_source_hbm,
    right_source_hbm,
    left_hbm,
    right_hbm,
    out,
    energies,
    weights,
    indices,
    levels,
    source,
    left,
    right,
    left_turned,
    right_turned,
    rows,
    first,
    middle,
    density,
    partial,
    gathered,
    forward_in,
    forward_out,
    backward_in,
    backward_out,
    load_sem,
    swap_send,
    swap_recv,
    forward_send,
    forward_recv,
    backward_send,
    backward_recv,
    gather_send,
    gather_recv,
):
    count = indices.shape[0]
    modes = source.shape[1]
    orbitals = levels.shape[1]
    spot = lax.axis_index("slab")
    team = lax.axis_index("energy")
    chips = chain // 2
    chip = spot // 2
    core = spot % 2
    twin = spot + 1 - 2 * core
    lowest = chip == 0
    highest = chip == chips - 1

    def load(origin, target, place):
        return pltpu.make_async_copy(origin, target, load_sem.at[place])

    left_load = load(left_source_hbm, source, 0)
    right_load = load(right_source_hbm, source, 0)
    bases = [
        load(right_hbm.at[0], right.at[core], 1),
        load(left_hbm.at[0], left.at[core], 2),
    ]
    tables = [
        load(energies_hbm, energies, 3),
        load(weights_hbm, weights, 4),
        load(indices_hbm, indices, 5),
        load(levels_hbm, levels, 6),
    ]
    pl.when(spot == 0)(left_load.start)
    pl.when(spot == chain - 1)(right_load.start)
    for item in bases + tables:
        item.start()

    barrier = pltpu.get_barrier_semaphore()

    def greet(place):
        pl.semaphore_signal(barrier, inc=1, device_id=place, device_id_type=MESH)

    def greet_chip(other):
        greet({"slab": 2 * other})
        greet({"slab": 2 * other + 1})

    pl.when(chip > 0)(lambda: greet_chip(chip - 1))
    pl.when(chip < chips - 1)(lambda: greet_chip(chip + 1))
    greet({"slab": twin})
    for step in range(1, teams):
        peer = lax.rem(team + step, teams)
        greet({"energy": peer})
        greet({"energy": peer, "slab": twin})

    density[...] = jnp.zeros_like(density)
    for item in tables:
        item.wait()
    rows[core] = levels[pl.ds(potential[0], 1), :]

    at_end = lowest | highest

    def swap(origin, target, place):
        return pltpu.make_async_remote_copy(
            src_ref=origin,
            dst_ref=target,
            send_sem=swap_send.at[place],
            recv_sem=swap_recv.at[place],
            device_id={"slab": twin},
            device_id_type=MESH,
        )

    swaps = [
        swap(rows.at[core], rows.at[core], 0),
        swap(right_hbm.at[0], right.at[core], 1),
        swap(left_hbm.at[0], left.at[core], 2),
    ]
    def settle_bases():
        for item in bases:
            item.wait()

    def start_swaps():
        for item in swaps:
            item.start()

    def settle_swaps():
        for item in swaps:
            item.wait_recv()

    def turned_source():
        return source[...].astype(jnp.float32).T.astype(jnp.bfloat16)

    def turn_bases(side):
        left_turned[side] = left[side].T
        right_turned[side] = right[side].T

    pl.when(at_end)(settle_bases)

    @pl.when(spot == 0)
    def _():
        left_load.wait()
        first[...] = dot(turned_source(), right[0], NT)

    @pl.when(spot == chain - 1)
    def _():
        right_load.wait()
        first[...] = dot(turned_source(), left[1], NN)

    pl.when(spot == 1)(lambda: turn_bases(1))

    pl.when(at_end)(lambda: pl.semaphore_wait(barrier, 2 * teams + 1))
    pl.when(jnp.logical_not(at_end))(lambda: pl.semaphore_wait(barrier, 2 * teams + 3))

    @pl.when(jnp.logical_not(at_end))
    def _():
        start_swaps()
        settle_bases()
        turn_bases(core)
        settle_swaps()
        turn_bases(1 - core)

    def copy_of(origin, target, send, recv, slot, place):
        return pltpu.make_async_remote_copy(
            src_ref=origin.at[slot],
            dst_ref=target.at[slot],
            send_sem=send.at[slot],
            recv_sem=recv.at[slot],
            device_id={"slab": place},
            device_id_type=MESH,
        )

    forward_copy = functools.partial(
        copy_of, forward_out, forward_in, forward_send, forward_recv
    )
    backward_copy = functools.partial(
        copy_of, backward_out, backward_in, backward_send, backward_recv
    )

    def scaled(mixed, slot, side):
        scale = 1.0 / (energies[indices[slot]] - rows[side])
        return (scale * mixed).astype(jnp.bfloat16)

    def count_in(state, slot, side):
        weight = weights[indices[slot]] / (count * teams * modes)
        squared = state[...].astype(jnp.float32) ** 2
        part = jnp.sum(squared.reshape(modes // 8, 8, orbitals), axis=0)
        density[side] += weight * part

    def down(state, slot, side):
        mixed = dot(state, right_turned[side], NN)
        return dot(scaled(mixed, slot, side), left_turned[side], NN).astype(jnp.bfloat16)

    def up(state, slot, side):
        mixed = dot(state, left[side], NN)
        return dot(scaled(mixed, slot, side), right[side], NN).astype(jnp.bfloat16)

    def each(body):
        def step(slot, carry):
            body(slot)
            return carry

        lax.fori_loop(0, count, step, 0)

    def mine(body):
        each(lambda slot: pl.when(slot % 2 == core)(lambda: body(slot)))

    def sweep(begin, end, near, far, copy, state_in, state_out, advance, opening, start, onward):
        @pl.when(begin & (core == near))
        def _():
            def body(slot):
                mixed = scaled(first[...], slot, near)
                state_out[slot] = opening(mixed).astype(jnp.bfloat16)
                copy(slot, twin).start()
                count_in(state_out.at[slot], slot, near)

            each(body)

        @pl.when(begin & (core == far))
        def _():
            def body(slot):
                copy(slot, twin).wait_recv()
                state_out[slot] = advance(state_in[slot], slot, far)
                copy(slot, start + slot % 2).start()
                count_in(state_out.at[slot], slot, far)

            each(body)

        @pl.when(jnp.logical_not(begin))
        def _():
            def body(slot):
                copy(slot, twin).wait_recv()
                middle[...] = advance(state_in[slot], slot, near)
                state_out[slot] = advance(middle[...], slot, far)
                pl.when(jnp.logical_not(end))(lambda: copy(slot, onward).start())
                count_in(middle, slot, near)
                count_in(state_out.at[slot], slot, far)

            mine(body)

    def forward():
        sweep(
            lowest, highest, 0, 1, forward_copy, forward_in, forward_out, down,
            lambda mixed: dot(mixed, left[0], NT), 2, spot + 2,
        )

    def backward():
        sweep(
            highest, lowest, 1, 0, backward_copy, backward_in, backward_out, up,
            lambda mixed: dot(mixed, right[1], NN), chain - 4, spot - 2,
        )

    upper = chip >= chips // 2
    pl.when(jnp.logical_not(upper))(forward)

    @pl.when(lowest)
    def _():
        start_swaps()
        settle_swaps()

    backward()

    @pl.when(highest)
    def _():
        start_swaps()
        settle_swaps()
        turn_bases(0)
        turn_bases(1)

    pl.when(upper)(forward)

    gathered[2 * team + core] = jnp.sum(density[core], axis=0, keepdims=True)
    partial[...] = jnp.sum(density[1 - core], axis=0, keepdims=True)

    def share(step, across):
        peer = lax.rem(team + step, teams)
        place = teams * across + step
        return pltpu.make_async_remote_copy(
            src_ref=partial if across else gathered.at[2 * team + core],
            dst_ref=gathered.at[2 * team + core],
            send_sem=gather_send.at[place],
            recv_sem=gather_recv.at[place],
            device_id={"energy": peer, "slab": twin if across else spot},
            device_id_type=MESH,
        )

    shares = [share(step, 1) for step in range(teams)]
    shares += [share(step, 0) for step in range(1, teams)]
    for item in shares:
        item.start()

    def sent(copy, begin, end):
        pl.when(begin)(lambda: each(lambda slot: copy(slot, twin).wait_send()))
        pl.when(jnp.logical_not(begin | end))(
            lambda: mine(lambda slot: copy(slot, twin).wait_send())
        )

    sent(forward_copy, lowest, highest)
    sent(backward_copy, highest, lowest)
    for item in swaps:
        item.wait_send()
    for item in shares:
        item.wait()
    total = gathered[0]
    for member in range(1, 2 * teams):
        total += gathered[member]
    out[...] = total


def local(
    teams,
    chain,
    left_basis,
    right_basis,
    potential_index,
    levels,
    energy_values,
    energy_weights,
    energy_index,
    left_source,
    right_source,
):
    count = energy_index.shape[0]
    orbitals = left_basis.shape[1]
    modes = left_source.shape[1]
    block = (count, modes, orbitals)
    outside = pl.BlockSpec(memory_space=pltpu.HBM)
    square = pltpu.VMEM((2, orbitals, orbitals), jnp.bfloat16)
    copies = pltpu.SemaphoreType.DMA((count,))
    return pl.pallas_call(
        functools.partial(kernel, chain, teams),
        out_shape=jax.ShapeDtypeStruct((1, orbitals), jnp.float32),
        in_specs=[pl.BlockSpec(memory_space=pltpu.SMEM)] + [outside] * 8,
        out_specs=pl.BlockSpec(memory_space=pltpu.VMEM),
        scratch_shapes=[
            pltpu.SMEM(energy_values.shape, jnp.float32),
            pltpu.SMEM(energy_weights.shape, jnp.float32),
            pltpu.SMEM(energy_index.shape, jnp.int32),
            pltpu.VMEM(levels.shape, jnp.float32),
            pltpu.VMEM(left_source.shape, jnp.bfloat16),
            square,
            square,
            square,
            square,
            pltpu.VMEM((2, 1, orbitals), jnp.float32),
            pltpu.VMEM((modes, orbitals), jnp.float32),
            pltpu.VMEM((modes, orbitals), jnp.bfloat16),
            pltpu.VMEM((2, 8, orbitals), jnp.float32),
            pltpu.VMEM((1, orbitals), jnp.float32),
            pltpu.VMEM((2 * teams, 1, orbitals), jnp.float32),
            pltpu.VMEM(block, jnp.bfloat16),
            pltpu.VMEM(block, jnp.bfloat16),
            pltpu.VMEM(block, jnp.bfloat16),
            pltpu.VMEM(block, jnp.bfloat16),
            pltpu.SemaphoreType.DMA((7,)),
            pltpu.SemaphoreType.DMA((3,)),
            pltpu.SemaphoreType.DMA((3,)),
            copies,
            copies,
            copies,
            copies,
            pltpu.SemaphoreType.DMA((2 * teams,)),
            pltpu.SemaphoreType.DMA((2 * teams,)),
        ],
        compiler_params=pltpu.CompilerParams(
            collective_id=0, has_side_effects=True, vmem_limit_bytes=63 << 20
        ),
    )(
        potential_index,
        energy_values,
        energy_weights,
        energy_index,
        levels,
        left_source,
        right_source,
        left_basis,
        right_basis,
    )


def solution(mesh):
    placed = (
        P("slab", None, None),
        P("slab", None, None),
        P("slab"),
        P(),
        P(),
        P(),
        P("energy"),
        P(),
        P(),
    )
    return jax.shard_map(
        functools.partial(local, mesh.shape["energy"], mesh.shape["slab"]),
        mesh=mesh,
        in_specs=placed,
        out_specs=P("slab", None),
        check_vma=False,
    )
```

```python
import functools

import jax
import jax.numpy as jnp
from jax import lax
from jax.experimental import pallas as pl
from jax.experimental.pallas import tpu as pltpu
from jax.sharding import PartitionSpec as P

MESH = pl.DeviceIdType.MESH
NN = (((1,), (0,)), ((), ()))
NT = (((1,), (1,)), ((), ()))


def dot(a, b, dims):
    return lax.dot_general(a, b, dims, preferred_element_type=jnp.float32)


def kernel(
    chain,
    teams,
    potential,
    energies_hbm,
    weights_hbm,
    indices_hbm,
    levels_hbm,
    left_source_hbm,
    right_source_hbm,
    left_hbm,
    right_hbm,
    out,
    energies,
    weights,
    indices,
    levels,
    source,
    left,
    right,
    left_turned,
    right_turned,
    rows,
    first,
    middle,
    density,
    partial,
    gathered,
    forward_in,
    forward_out,
    backward_in,
    backward_out,
    load_sem,
    swap_send,
    swap_recv,
    forward_send,
    forward_recv,
    backward_send,
    backward_recv,
    gather_send,
    gather_recv,
):
    count = indices.shape[0]
    modes = source.shape[1]
    orbitals = levels.shape[1]
    spot = lax.axis_index("slab")
    team = lax.axis_index("energy")
    chips = chain // 2
    chip = spot // 2
    core = spot % 2
    twin = spot + 1 - 2 * core
    lowest = chip == 0
    highest = chip == chips - 1

    def load(origin, target, place):
        return pltpu.make_async_copy(origin, target, load_sem.at[place])

    left_load = load(left_source_hbm, source, 0)
    right_load = load(right_source_hbm, source, 0)
    bases = [
        load(right_hbm.at[0], right.at[core], 1),
        load(left_hbm.at[0], left.at[core], 2),
    ]
    tables = [
        load(energies_hbm, energies, 3),
        load(weights_hbm, weights, 4),
        load(indices_hbm, indices, 5),
        load(levels_hbm, levels, 6),
    ]
    pl.when(spot == 0)(left_load.start)
    pl.when(spot == chain - 1)(right_load.start)
    for item in bases + tables:
        item.start()

    barrier = pltpu.get_barrier_semaphore()

    def greet(place):
        pl.semaphore_signal(barrier, inc=1, device_id=place, device_id_type=MESH)

    def greet_chip(other):
        greet({"slab": 2 * other})
        greet({"slab": 2 * other + 1})

    pl.when(chip > 0)(lambda: greet_chip(chip - 1))
    pl.when(chip < chips - 1)(lambda: greet_chip(chip + 1))
    greet({"slab": twin})
    for step in range(1, teams):
        peer = lax.rem(team + step, teams)
        greet({"energy": peer})
        greet({"energy": peer, "slab": twin})

    density[...] = jnp.zeros_like(density)
    for item in tables:
        item.wait()
    rows[core] = levels[pl.ds(potential[0], 1), :]

    at_end = lowest | highest

    def swap(origin, target, place):
        return pltpu.make_async_remote_copy(
            src_ref=origin,
            dst_ref=target,
            send_sem=swap_send.at[place],
            recv_sem=swap_recv.at[place],
            device_id={"slab": twin},
            device_id_type=MESH,
        )

    swaps = [
        swap(rows.at[core], rows.at[core], 0),
        swap(right_hbm.at[0], right.at[core], 1),
        swap(left_hbm.at[0], left.at[core], 2),
    ]
    def settle_bases():
        for item in bases:
            item.wait()

    def start_swaps():
        for item in swaps:
            item.start()

    def settle_swaps():
        for item in swaps:
            item.wait_recv()

    def turned_source():
        return source[...].astype(jnp.float32).T.astype(jnp.bfloat16)

    def turn_bases(side):
        left_turned[side] = left[side].T
        right_turned[side] = right[side].T

    pl.when(at_end)(settle_bases)

    @pl.when(spot == 0)
    def _():
        left_load.wait()
        first[...] = dot(turned_source(), right[0], NT)

    @pl.when(spot == chain - 1)
    def _():
        right_load.wait()
        first[...] = dot(turned_source(), left[1], NN)

    pl.when(spot == 1)(lambda: turn_bases(1))

    pl.when(at_end)(lambda: pl.semaphore_wait(barrier, 2 * teams + 1))
    pl.when(jnp.logical_not(at_end))(lambda: pl.semaphore_wait(barrier, 2 * teams + 3))

    @pl.when(jnp.logical_not(at_end))
    def _():
        start_swaps()
        settle_bases()
        turn_bases(core)
        settle_swaps()
        turn_bases(1 - core)

    def copy_of(origin, target, send, recv, slot, place):
        return pltpu.make_async_remote_copy(
            src_ref=origin.at[slot],
            dst_ref=target.at[slot],
            send_sem=send.at[slot],
            recv_sem=recv.at[slot],
            device_id={"slab": place},
            device_id_type=MESH,
        )

    forward_copy = functools.partial(
        copy_of, forward_out, forward_in, forward_send, forward_recv
    )
    backward_copy = functools.partial(
        copy_of, backward_out, backward_in, backward_send, backward_recv
    )

    def scaled(mixed, slot, side):
        scale = 1.0 / (energies[indices[slot]] - rows[side])
        return (scale * mixed).astype(jnp.bfloat16)

    def count_in(state, slot, side):
        weight = weights[indices[slot]] / (count * teams * modes)
        squared = state[...].astype(jnp.float32) ** 2
        part = jnp.sum(squared.reshape(modes // 8, 8, orbitals), axis=0)
        density[side] += weight * part

    def down(state, slot, side):
        mixed = dot(state, right_turned[side], NN)
        return dot(scaled(mixed, slot, side), left_turned[side], NN).astype(jnp.bfloat16)

    def up(state, slot, side):
        mixed = dot(state, left[side], NN)
        return dot(scaled(mixed, slot, side), right[side], NN).astype(jnp.bfloat16)

    def each(body):
        def step(slot, carry):
            body(slot)
            return carry

        lax.fori_loop(0, count, step, 0)

    def mine(body):
        each(lambda slot: pl.when(slot % 2 == core)(lambda: body(slot)))

    def sweep(begin, end, near, far, copy, state_in, state_out, advance, opening, start, onward):
        @pl.when(begin & (core == near))
        def _():
            def body(slot):
                mixed = scaled(first[...], slot, near)
                state_out[slot] = opening(mixed).astype(jnp.bfloat16)
                copy(slot, twin).start()
                count_in(state_out.at[slot], slot, near)

            each(body)

        @pl.when(begin & (core == far))
        def _():
            def body(slot):
                copy(slot, twin).wait_recv()
                state_out[slot] = advance(state_in[slot], slot, far)
                copy(slot, start + slot % 2).start()
                count_in(state_out.at[slot], slot, far)

            each(body)

        @pl.when(jnp.logical_not(begin))
        def _():
            def body(slot):
                copy(slot, twin).wait_recv()
                middle[...] = advance(state_in[slot], slot, near)
                count_in(middle, slot, near)
                state_out[slot] = advance(middle[...], slot, far)
                pl.when(jnp.logical_not(end))(lambda: copy(slot, onward).start())
                count_in(state_out.at[slot], slot, far)

            mine(body)

    def forward():
        sweep(
            lowest, highest, 0, 1, forward_copy, forward_in, forward_out, down,
            lambda mixed: dot(mixed, left[0], NT), 2, spot + 2,
        )

    def backward():
        sweep(
            highest, lowest, 1, 0, backward_copy, backward_in, backward_out, up,
            lambda mixed: dot(mixed, right[1], NN), chain - 4, spot - 2,
        )

    upper = chip >= chips // 2
    pl.when(jnp.logical_not(upper))(forward)

    @pl.when(lowest)
    def _():
        start_swaps()
        settle_swaps()

    backward()

    @pl.when(highest)
    def _():
        start_swaps()
        settle_swaps()
        turn_bases(0)
        turn_bases(1)

    pl.when(upper)(forward)

    gathered[2 * team + core] = jnp.sum(density[core], axis=0, keepdims=True)
    partial[...] = jnp.sum(density[1 - core], axis=0, keepdims=True)

    def share(step, across):
        peer = lax.rem(team + step, teams)
        place = teams * across + step
        return pltpu.make_async_remote_copy(
            src_ref=partial if across else gathered.at[2 * team + core],
            dst_ref=gathered.at[2 * team + core],
            send_sem=gather_send.at[place],
            recv_sem=gather_recv.at[place],
            device_id={"energy": peer, "slab": twin if across else spot},
            device_id_type=MESH,
        )

    shares = [share(step, 1) for step in range(teams)]
    shares += [share(step, 0) for step in range(1, teams)]
    for item in shares:
        item.start()

    def sent(copy, begin, end):
        pl.when(begin)(lambda: each(lambda slot: copy(slot, twin).wait_send()))
        pl.when(jnp.logical_not(begin | end))(
            lambda: mine(lambda slot: copy(slot, twin).wait_send())
        )

    sent(forward_copy, lowest, highest)
    sent(backward_copy, highest, lowest)
    for item in swaps:
        item.wait_send()
    for item in shares:
        item.wait()
    total = gathered[0]
    for member in range(1, 2 * teams):
        total += gathered[member]
    out[...] = total


def local(
    teams,
    chain,
    left_basis,
    right_basis,
    potential_index,
    levels,
    energy_values,
    energy_weights,
    energy_index,
    left_source,
    right_source,
):
    count = energy_index.shape[0]
    orbitals = left_basis.shape[1]
    modes = left_source.shape[1]
    block = (count, modes, orbitals)
    outside = pl.BlockSpec(memory_space=pltpu.HBM)
    square = pltpu.VMEM((2, orbitals, orbitals), jnp.bfloat16)
    copies = pltpu.SemaphoreType.DMA((count,))
    return pl.pallas_call(
        functools.partial(kernel, chain, teams),
        out_shape=jax.ShapeDtypeStruct((1, orbitals), jnp.float32),
        in_specs=[pl.BlockSpec(memory_space=pltpu.SMEM)] + [outside] * 8,
        out_specs=pl.BlockSpec(memory_space=pltpu.VMEM),
        scratch_shapes=[
            pltpu.SMEM(energy_values.shape, jnp.float32),
            pltpu.SMEM(energy_weights.shape, jnp.float32),
            pltpu.SMEM(energy_index.shape, jnp.int32),
            pltpu.VMEM(levels.shape, jnp.float32),
            pltpu.VMEM(left_source.shape, jnp.bfloat16),
            square,
            square,
            square,
            square,
            pltpu.VMEM((2, 1, orbitals), jnp.float32),
            pltpu.VMEM((modes, orbitals), jnp.float32),
            pltpu.VMEM((modes, orbitals), jnp.bfloat16),
            pltpu.VMEM((2, 8, orbitals), jnp.float32),
            pltpu.VMEM((1, orbitals), jnp.float32),
            pltpu.VMEM((2 * teams, 1, orbitals), jnp.float32),
            pltpu.VMEM(block, jnp.bfloat16),
            pltpu.VMEM(block, jnp.bfloat16),
            pltpu.VMEM(block, jnp.bfloat16),
            pltpu.VMEM(block, jnp.bfloat16),
            pltpu.SemaphoreType.DMA((7,)),
            pltpu.SemaphoreType.DMA((3,)),
            pltpu.SemaphoreType.DMA((3,)),
            copies,
            copies,
            copies,
            copies,
            pltpu.SemaphoreType.DMA((2 * teams,)),
            pltpu.SemaphoreType.DMA((2 * teams,)),
        ],
        compiler_params=pltpu.CompilerParams(
            collective_id=0, has_side_effects=True, vmem_limit_bytes=63 << 20
        ),
    )(
        potential_index,
        energy_values,
        energy_weights,
        energy_index,
        levels,
        left_source,
        right_source,
        left_basis,
        right_basis,
    )


def solution(mesh):
    placed = (
        P("slab", None, None),
        P("slab", None, None),
        P("slab"),
        P(),
        P(),
        P(),
        P("energy"),
        P(),
        P(),
    )
    return jax.shard_map(
        functools.partial(local, mesh.shape["energy"], mesh.shape["slab"]),
        mesh=mesh,
        in_specs=placed,
        out_specs=P("slab", None),
        check_vma=False,
    )
```
